32 devices in a mesh: dp: 16 (over z, x, core), shard: 2 (over y).
Axes of the slice: x: 2, y: 2, z: 4, core: 2. Of those that a mesh axis runs over, the one named last changes fastest.
Arguments:
- tokens: bfloat16 [4096, 1088], P(('dp', 'shard')), may hold values from -6 to 6
- seq_ends: int32 [32, 3], P(('dp', 'shard')), may hold values from 0 to 128, as said below
- attn_weight: bfloat16 [1, 4352, 1088], P(None, ('dp', 'shard'))
- up_weight: bfloat16 [1, 4352, 1088], P(None, ('dp', 'shard')), may hold values from -0.1875 to 0.1875
- down_weight: bfloat16 [1, 4352, 1088], P(None, ('dp', 'shard')), may hold values from -0.09375 to 0.09375
- vectors: bfloat16 [1, 13056], P(None, ('dp', 'shard'))
- cotangent: bfloat16 [4096, 1088], P(('dp', 'shard')), may hold values from -6 to 6
Outputs:
- output: bfloat16 [4096, 1088], P(('dp', 'shard'))
- grad_tokens: float32 [4096, 1088], P(('dp', 'shard'))
- grad_attn: float32 [1, 4352, 1088], P(None, ('dp', 'shard'))
- grad_up: float32 [1, 4352, 1088], P(None, ('dp', 'shard'))
- grad_down: float32 [1, 4352, 1088], P(None, ('dp', 'shard'))
- grad_vectors: float32 [1, 13056], P(None, ('dp', 'shard'))
The draws below stay inside these ranges and needn't reach their ends.
Inputs may be any that keep to these rules, and one draw needn't show every extreme that they name: `seq_ends`: each row lists non-decreasing end offsets of the sequences packed into one device's 128 slots; slots from the row's last end onward form one more segment.
All inputs are finite; a program needn't handle non-finite values.
Results may differ from the reference program's by a relative error of at most 0.0089.
Values may be sent and summed in bfloat16 or wider, within the bound.
A program may use at most 192 MiB of HBM per device.

```python
import jax
import jax.numpy as jnp
from jax import lax

D = 1088
FF = 4352
HEAD_DIM = 64
LAYERS = 1
CAP = 128
SEQ_DEV = 3
GROUPS = 32
TOKENS = 4096


def draw_seq_ends(key, part):
    raw_ends = jax.random.randint(key, (GROUPS, SEQ_DEV), 0, CAP + 1)
    ordered = jnp.sort(raw_ends, axis=1)
    ordered = ordered.at[0, SEQ_DEV - 1].set(CAP)
    ordered = ordered.at[1, 0].set(0)
    return ordered.astype(jnp.int32)


def draw_attn_weight(key, part):
    full_shape = (LAYERS, 4 * D, D)
    sample = jax.random.normal(key, full_shape, jnp.float32)
    row_index = jnp.arange(4 * D)[None, :, None]
    factor = jnp.where(row_index < 3 * D, D ** (-0.5), 4.0 * D ** (-0.5))
    return (sample * factor).astype(jnp.bfloat16)


def draw_vectors(key, part):
    length_all = 8 * D + FF
    key_first, key_second = jax.random.split(key)
    spread = jax.random.uniform(key_first, (LAYERS, length_all), jnp.float32, -1.0, 1.0)
    normal_part = jax.random.normal(key_second, (LAYERS, length_all), jnp.float32)
    slot_index = jnp.arange(length_all)[None, :] // D
    is_gain = (slot_index == 0) | (slot_index == 5)
    return jnp.where(is_gain, 1.0 + 0.3 * spread, 0.3 * normal_part).astype(jnp.bfloat16)


def levels(rng, shape, cuts, low, high):
    level = 1.0
    for dim, shards_of in cuts:
        draws = jax.random.uniform(jax.random.fold_in(jax.random.fold_in(rng, 6), dim), (shards_of,), jnp.float32, low / len(cuts), high / len(cuts))
        level = level * jnp.repeat(jnp.exp(draws), shape[dim] // shards_of).reshape((-1,) + (1,) * (len(shape) - 1 - dim))
    return level


def scatter_about(stream_key, shape, width, bound, cuts=(), held_as=jnp.bfloat16):
    array = width * jax.random.normal(stream_key, shape, jnp.float32)
    if cuts:
        array = array * levels(stream_key, shape, cuts, -0.22, 0.18)
    return jnp.clip(array, -bound, bound).astype(held_as)


def setup_inputs(seed: int = 0) -> dict:
    key_list = jax.random.split(jax.random.key(seed), 8)
    tokens = scatter_about(key_list[0], (TOKENS, D), 1.0, 6.0, ((0, 32),))
    seq_ends = draw_seq_ends(jax.random.fold_in(key_list[7], 71), 0)
    attn_weight = draw_attn_weight(jax.random.fold_in(key_list[7], 71), 0)
    up_weight = scatter_about(key_list[3], (LAYERS, FF, D), D ** -0.5, 0.1875, ((1, 32),))
    down_weight = scatter_about(key_list[4], (LAYERS, FF, D), FF ** -0.5, 0.09375, ((1, 32),))
    vectors = draw_vectors(jax.random.fold_in(key_list[7], 71), 0)
    cotangent = scatter_about(key_list[6], (TOKENS, D), 1.0, 6.0, ((0, 32),))
    return {"tokens": tokens, "seq_ends": seq_ends, "attn_weight": attn_weight, "up_weight": up_weight, "down_weight": down_weight, "vectors": vectors, "cotangent": cotangent}


EPS = 1e-05

def layer_norm(values, gain, shift):
    average = lax.optimization_barrier(jnp.mean(values, axis=-1, keepdims=True))
    centred = values - average
    variance = lax.optimization_barrier(jnp.mean(centred * centred, axis=-1, keepdims=True))
    return centred * lax.rsqrt(variance + EPS) * gain + shift

def gelu_tanh(values):
    return 0.5 * values * (1.0 + jnp.tanh(0.7978845608028654 * (values + 0.044715 * values * values * values)))

def contract_last(left, right):
    return lax.dot_general(left, right, (((1,), (1,)), ((), ())), preferred_element_type=jnp.float32)

def contract_first(left, right):
    return lax.dot_general(left, right, (((0,), (0,)), ((), ())), preferred_element_type=jnp.float32)

def head_product(form, left, right):
    return jnp.einsum(form, left.astype(jnp.float32), right.astype(jnp.float32))

def causal_mask(ends_row, slot_count):
    positions = jnp.arange(slot_count, dtype=jnp.int32)
    segment = lax.optimization_barrier(jnp.sum((ends_row[None, :] <= positions[:, None]).astype(jnp.int32), axis=1))
    return (segment[:, None] == segment[None, :]) & (positions[None, :] <= positions[:, None])

def split_vectors(vectors, model_width):
    vector_f32 = vectors.astype(jnp.float32)
    parts_list = [vector_f32[slot_idx * model_width:(slot_idx + 1) * model_width] for slot_idx in range(8)]
    return parts_list + [vector_f32[8 * model_width:]]

def forward_layer(hidden, params, allowed):
    attn_part, up_part, down_part, vector_part = params
    model_width = attn_part.shape[1]
    head_count = model_width // HEAD_DIM
    row_count = hidden.shape[0]
    gain_one, shift_one, query_bias, value_bias, out_bias, gain_two, shift_two, down_bias, up_bias = split_vectors(vector_part, model_width)
    normed_one = layer_norm(hidden, gain_one, shift_one).astype(jnp.bfloat16)
    projected = contract_last(normed_one, attn_part[:3 * model_width])
    query_heads = ((projected[:, :model_width] + query_bias) * HEAD_DIM ** (-0.5)).astype(jnp.bfloat16).reshape(row_count, head_count, HEAD_DIM)
    key_heads = projected[:, model_width:2 * model_width].astype(jnp.bfloat16).reshape(row_count, head_count, HEAD_DIM)
    value_heads = (projected[:, 2 * model_width:] + value_bias).astype(jnp.bfloat16).reshape(row_count, head_count, HEAD_DIM)
    scores = jnp.where(allowed[None], head_product('qhc,khc->hqk', query_heads, key_heads), -1e+30)
    log_total = jnp.log(lax.optimization_barrier(jnp.sum(jnp.exp(scores), axis=-1)))
    weights = jnp.exp(scores - log_total[..., None]).astype(jnp.bfloat16)
    context = head_product('hqk,khc->qhc', weights, value_heads).reshape(row_count, model_width).astype(jnp.bfloat16)
    after_attn = hidden + jnp.dot(context, attn_part[3 * model_width:], preferred_element_type=jnp.float32) + out_bias
    normed_two = layer_norm(after_attn, gain_two, shift_two).astype(jnp.bfloat16)
    pre_act = contract_last(normed_two, up_part) + up_bias
    activated = gelu_tanh(pre_act).astype(jnp.bfloat16)
    result = after_attn + jnp.dot(activated, down_part, preferred_element_type=jnp.float32) + down_bias
    saved_acts = (hidden, normed_one, query_heads, key_heads, value_heads, log_total, context, after_attn, normed_two, pre_act, activated)
    return (result, saved_acts)

def backward_layer(upstream, params, saved_acts, allowed):
    attn_part, up_part, down_part, vector_part = params
    hidden, normed_one, query_heads, key_heads, value_heads, log_total, context, after_attn, normed_two, pre_act, activated = saved_acts
    model_width = attn_part.shape[1]
    head_count = model_width // HEAD_DIM
    row_count = hidden.shape[0]
    gain_one, shift_one, query_bias, value_bias, out_bias, gain_two, shift_two, down_bias, up_bias = split_vectors(vector_part, model_width)
    upstream_bf = upstream.astype(jnp.bfloat16)
    grad_down_w = contract_first(activated, upstream_bf)
    grad_down_bias = lax.optimization_barrier(jnp.sum(upstream, axis=0))
    grad_act = contract_last(upstream_bf, down_part)
    grad_pre = jax.vjp(gelu_tanh, pre_act)[1](grad_act)[0]
    grad_up_bias = lax.optimization_barrier(jnp.sum(grad_pre, axis=0))
    grad_pre_bf = grad_pre.astype(jnp.bfloat16)
    grad_up_w = contract_first(grad_pre_bf, normed_two)
    grad_normed_two = jnp.dot(grad_pre_bf, up_part, preferred_element_type=jnp.float32)
    back_two = jax.vjp(layer_norm, after_attn, gain_two, shift_two)[1]
    grad_mid, grad_gain_two, grad_shift_two = back_two(grad_normed_two)
    grad_mid = upstream + grad_mid
    grad_out_bias = lax.optimization_barrier(jnp.sum(grad_mid, axis=0))
    grad_mid_bf = grad_mid.astype(jnp.bfloat16)
    grad_out_w = contract_first(context, grad_mid_bf)
    grad_context = contract_last(grad_mid_bf, attn_part[3 * model_width:]).astype(jnp.bfloat16).reshape(row_count, head_count, HEAD_DIM)
    scores = jnp.where(allowed[None], head_product('qhc,khc->hqk', query_heads, key_heads), -1e+30)
    probs_f32 = jnp.exp(scores - log_total[..., None])
    probs_bf = probs_f32.astype(jnp.bfloat16)
    grad_values = head_product('hqk,qhc->khc', probs_bf, grad_context).reshape(row_count, model_width)
    grad_probs = head_product('qhc,khc->hqk', grad_context, value_heads)
    row_dot = lax.optimization_barrier(jnp.sum(probs_f32 * grad_probs, axis=-1, keepdims=True))
    grad_scores = (probs_f32 * (grad_probs - row_dot)).astype(jnp.bfloat16)
    grad_query = head_product('hqk,khc->qhc', grad_scores, key_heads).reshape(row_count, model_width) * HEAD_DIM ** (-0.5)
    grad_keys = head_product('hqk,qhc->khc', grad_scores, query_heads).reshape(row_count, model_width)
    grad_query_bias = lax.optimization_barrier(jnp.sum(grad_query, axis=0))
    grad_value_bias = lax.optimization_barrier(jnp.sum(grad_values, axis=0))
    grad_proj = jnp.concatenate([grad_query, grad_keys, grad_values], axis=1).astype(jnp.bfloat16)
    grad_qkv_w = contract_first(grad_proj, normed_one)
    grad_normed_one = jnp.dot(grad_proj, attn_part[:3 * model_width], preferred_element_type=jnp.float32)
    back_one = jax.vjp(layer_norm, hidden, gain_one, shift_one)[1]
    grad_below, grad_gain_one, grad_shift_one = back_one(grad_normed_one)
    grad_below = grad_mid + grad_below
    grad_attn_w = jnp.concatenate([grad_qkv_w, grad_out_w], axis=0)
    grad_vector = jnp.concatenate([grad_gain_one, grad_shift_one, grad_query_bias, grad_value_bias, grad_out_bias, grad_gain_two, grad_shift_two, grad_down_bias, grad_up_bias])
    return (grad_below, grad_attn_w, grad_up_w, grad_down_w, grad_vector)

def reference(tokens, seq_ends, attn_weight, up_weight, down_weight, vectors, cotangent):
    batch_width = 8

    def one_group(token_block, ends_row, cot_block):
        allowed = causal_mask(ends_row, CAP)
        hidden = token_block.astype(jnp.float32)
        saved_list = []
        for layer_idx in range(LAYERS):
            params = (attn_weight[layer_idx], up_weight[layer_idx], down_weight[layer_idx], vectors[layer_idx])
            hidden, saved_acts = forward_layer(hidden, params, allowed)
            saved_list.append(saved_acts)
        upstream = cot_block.astype(jnp.float32)
        grad_sets = [None] * LAYERS
        for layer_idx in reversed(range(LAYERS)):
            params = (attn_weight[layer_idx], up_weight[layer_idx], down_weight[layer_idx], vectors[layer_idx])
            results = backward_layer(upstream, params, saved_list[layer_idx], allowed)
            upstream = results[0]
            grad_sets[layer_idx] = results[1:]
        stacked = tuple((jnp.stack([grad_sets[layer_idx][member] for layer_idx in range(LAYERS)]) for member in range(4)))
        return (hidden.astype(jnp.bfloat16), upstream, stacked)
    token_blocks = tokens.reshape(GROUPS // batch_width, batch_width, CAP, D)
    ends_blocks = seq_ends.reshape(GROUPS // batch_width, batch_width, SEQ_DEV)
    cot_blocks = cotangent.reshape(GROUPS // batch_width, batch_width, CAP, D)

    def scan_step(totals, inputs):
        block_out, block_grad, block_params = jax.vmap(one_group)(*inputs)
        totals = tuple((total_now + lax.optimization_barrier(jnp.sum(piece_now, axis=0)) for total_now, piece_now in zip(totals, block_params)))
        return (totals, (block_out, block_grad))
    zero_totals = (jnp.zeros((LAYERS, 4 * D, D), jnp.float32), jnp.zeros((LAYERS, FF, D), jnp.float32), jnp.zeros((LAYERS, FF, D), jnp.float32), jnp.zeros((LAYERS, 8 * D + FF), jnp.float32))
    totals, (outputs, grads_in) = lax.scan(scan_step, zero_totals, (token_blocks, ends_blocks, cot_blocks))
    return (outputs.reshape(TOKENS, D), grads_in.reshape(TOKENS, D), totals[0], totals[1], totals[2], totals[3])
```

```python
import jax
import jax.numpy as jnp
from jax import lax
from jax.sharding import PartitionSpec as P

HEAD_DIM = 64


EPS = 1e-05
AXES = ("dp", "shard")


CORE, SIDE, ACROSS, LINE = 2, 1, 4, 8


def exchange(values, mask):
    pairs = [(source, source ^ mask) for source in range(lax.axis_size(AXES))]
    return lax.ppermute(values, AXES, pairs)


def gather_rows(values):
    return lax.all_gather(values, AXES, axis=0, tiled=True)


def scatter_rows(values):
    return lax.psum_scatter(values, AXES, scatter_dimension=0, tiled=True).astype(jnp.float32)


def relative_order(device_count):
    lines = list(range(0, device_count, LINE))
    orders = []
    for masks, steps in (
        (lines[: len(lines) // 2], (ACROSS, SIDE)),
        (lines[len(lines) // 2 :], (SIDE, ACROSS)),
    ):
        for step in steps:
            masks = masks + [mask ^ step for mask in masks]
        orders.append(masks)
    both = orders[0] + orders[1]
    return both + [mask ^ CORE for mask in both]


def gather_relative(block):
    device_count = lax.axis_size(AXES)
    lines = [block] + [exchange(block, mask) for mask in range(LINE, device_count, LINE)]
    pieces = []
    for members, steps in (
        (lines[: len(lines) // 2], (ACROSS, SIDE)),
        (lines[len(lines) // 2 :], (SIDE, ACROSS)),
    ):
        piece = jnp.concatenate(members, axis=0)
        for step in steps:
            piece = jnp.concatenate([piece, exchange(piece, step)], axis=0)
        pieces.append(piece)
    return pieces + [exchange(piece, CORE) for piece in pieces]


def add_rounded(left, right):
    return (left.astype(jnp.float32) + right.astype(jnp.float32)).astype(jnp.bfloat16)


def scatter_relative(left, right, block_rows):
    piece_rows = left.shape[1] // 4
    cuts = [left[:, piece * piece_rows : (piece + 1) * piece_rows] for piece in range(4)]
    away = [exchange(contract_first(cut, right).astype(jnp.bfloat16), CORE) for cut in cuts[2:]]
    lines = []
    for cut, received, steps in zip(cuts[:2], away, ((SIDE, ACROSS), (ACROSS, SIDE))):
        piece = (contract_first(cut, right) + received.astype(jnp.float32)).astype(jnp.bfloat16)
        for step in steps:
            half = piece.shape[0] // 2
            piece = add_rounded(piece[:half], exchange(piece[half:], step))
        lines += [
            piece[start : start + block_rows] for start in range(0, piece.shape[0], block_rows)
        ]
    total = lines[0].astype(jnp.float32)
    for index in range(1, len(lines)):
        total = total + exchange(lines[index], index * LINE).astype(jnp.float32)
    return total


def to_relative(values):
    device_count = lax.axis_size(AXES)
    order = jnp.array(relative_order(device_count), jnp.int32)
    blocks = values.reshape(device_count, -1)
    return blocks[order ^ lax.axis_index(AXES)].reshape(-1)


def from_relative(values):
    device_count = lax.axis_size(AXES)
    order = relative_order(device_count)
    place = jnp.array([order.index(mask) for mask in range(device_count)], jnp.int32)
    device = jnp.arange(device_count, dtype=jnp.int32) ^ lax.axis_index(AXES)
    return values.reshape(device_count, -1)[place[device]].reshape(-1)


def contract_last_pieces(left, pieces):
    return jnp.concatenate([contract_last(left, piece) for piece in pieces], axis=1)


def dot_pieces(left, pieces):
    rows = pieces[0].shape[0]
    total = None
    for index, piece in enumerate(pieces):
        term = jnp.dot(
            left[:, index * rows : (index + 1) * rows], piece, preferred_element_type=jnp.float32
        )
        total = term if total is None else total + term
    return total


def layer_norm(values, gain, shift):
    average = jnp.mean(values, axis=-1, keepdims=True)
    centred = values - average
    variance = jnp.mean(centred * centred, axis=-1, keepdims=True)
    return centred * lax.rsqrt(variance + EPS) * gain + shift


def gelu_tanh(values):
    return (
        0.5
        * values
        * (1.0 + jnp.tanh(0.7978845608028654 * (values + 0.044715 * values * values * values)))
    )


def contract_last(left, right):
    return lax.dot_general(
        left, right, (((1,), (1,)), ((), ())), preferred_element_type=jnp.float32
    )


def contract_first(left, right):
    return lax.dot_general(
        left, right, (((0,), (0,)), ((), ())), preferred_element_type=jnp.float32
    )


def head_product(form, left, right):
    return jnp.einsum(form, left, right, preferred_element_type=jnp.float32)


def causal_mask(ends_row, slot_count):
    positions = jnp.arange(slot_count, dtype=jnp.int32)
    segment = jnp.sum((ends_row[None, :] <= positions[:, None]).astype(jnp.int32), axis=1)
    return (segment[:, None] == segment[None, :]) & (positions[None, :] <= positions[:, None])


def split_vectors(vectors, model_width):
    vector_f32 = vectors.astype(jnp.float32)
    parts_list = [
        vector_f32[slot_idx * model_width : (slot_idx + 1) * model_width] for slot_idx in range(8)
    ]
    return parts_list + [vector_f32[8 * model_width :]]


def forward_layer(hidden, params, allowed):
    attn_part, up_part, down_part, vector_part = params
    model_width = attn_part.shape[1]
    head_count = model_width // HEAD_DIM
    row_count = hidden.shape[0]
    (
        gain_one,
        shift_one,
        query_bias,
        value_bias,
        out_bias,
        gain_two,
        shift_two,
        down_bias,
        up_bias,
    ) = split_vectors(vector_part, model_width)
    normed_one = layer_norm(hidden, gain_one, shift_one).astype(jnp.bfloat16)
    projected = contract_last(normed_one, attn_part[: 3 * model_width])
    query_heads = (
        ((projected[:, :model_width] + query_bias) * HEAD_DIM ** (-0.5))
        .astype(jnp.bfloat16)
        .reshape(row_count, head_count, HEAD_DIM)
    )
    key_heads = (
        projected[:, model_width : 2 * model_width]
        .astype(jnp.bfloat16)
        .reshape(row_count, head_count, HEAD_DIM)
    )
    value_heads = (
        (projected[:, 2 * model_width :] + value_bias)
        .astype(jnp.bfloat16)
        .reshape(row_count, head_count, HEAD_DIM)
    )
    scores = jnp.where(allowed[None], head_product("qhc,khc->hqk", query_heads, key_heads), -1e30)
    log_total = jnp.log(jnp.sum(jnp.exp(scores), axis=-1))
    weights = jnp.exp(scores - log_total[..., None]).astype(jnp.bfloat16)
    context = (
        head_product("hqk,khc->qhc", weights, value_heads)
        .reshape(row_count, model_width)
        .astype(jnp.bfloat16)
    )
    after_attn = (
        hidden
        + jnp.dot(context, attn_part[3 * model_width :], preferred_element_type=jnp.float32)
        + out_bias
    )
    normed_two = layer_norm(after_attn, gain_two, shift_two).astype(jnp.bfloat16)
    up_bias = to_relative(up_bias)
    pre_act = contract_last_pieces(normed_two, up_part) + up_bias
    activated = gelu_tanh(pre_act).astype(jnp.bfloat16)
    result = (
        after_attn + dot_pieces(activated, down_part) + down_bias
    )
    saved_acts = (
        hidden,
        normed_one,
        query_heads,
        key_heads,
        value_heads,
        log_total,
        context,
        after_attn,
        normed_two,
        pre_act,
        activated,
    )
    return (result, saved_acts)


def backward_layer(upstream, params, saved_acts, allowed):
    attn_part, up_part, down_part, vector_part = params
    (
        hidden,
        normed_one,
        query_heads,
        key_heads,
        value_heads,
        log_total,
        context,
        after_attn,
        normed_two,
        pre_act,
        activated,
    ) = saved_acts
    model_width = attn_part.shape[1]
    head_count = model_width // HEAD_DIM
    row_count = hidden.shape[0]
    (
        gain_one,
        shift_one,
        query_bias,
        value_bias,
        out_bias,
        gain_two,
        shift_two,
        down_bias,
        up_bias,
    ) = split_vectors(vector_part, model_width)
    device_count = lax.axis_size(AXES)
    block_rows = pre_act.shape[1] // device_count
    upstream_bf = upstream.astype(jnp.bfloat16)
    grad_down_w = scatter_relative(activated, upstream_bf, block_rows)
    grad_down_bias = jnp.sum(upstream, axis=0)
    grad_act = contract_last_pieces(upstream_bf, down_part)
    grad_pre = jax.vjp(gelu_tanh, pre_act)[1](grad_act)[0]
    grad_up_bias = from_relative(jnp.sum(grad_pre, axis=0))
    grad_pre_bf = grad_pre.astype(jnp.bfloat16)
    grad_up_w = scatter_relative(grad_pre_bf, normed_two, block_rows)
    grad_normed_two = dot_pieces(grad_pre_bf, up_part)
    back_two = jax.vjp(layer_norm, after_attn, gain_two, shift_two)[1]
    grad_mid, grad_gain_two, grad_shift_two = back_two(grad_normed_two)
    grad_mid = upstream + grad_mid
    grad_out_bias = jnp.sum(grad_mid, axis=0)
    grad_mid_bf = grad_mid.astype(jnp.bfloat16)
    grad_context = (
        contract_last(grad_mid_bf, attn_part[3 * model_width :])
        .astype(jnp.bfloat16)
        .reshape(row_count, head_count, HEAD_DIM)
    )
    scores = jnp.where(allowed[None], head_product("qhc,khc->hqk", query_heads, key_heads), -1e30)
    probs_f32 = jnp.exp(scores - log_total[..., None])
    probs_bf = probs_f32.astype(jnp.bfloat16)
    grad_values = head_product("hqk,qhc->khc", probs_bf, grad_context).reshape(
        row_count, model_width
    )
    grad_probs = head_product("qhc,khc->hqk", grad_context, value_heads)
    row_dot = jnp.sum(probs_f32 * grad_probs, axis=-1, keepdims=True)
    grad_scores = (probs_f32 * (grad_probs - row_dot)).astype(jnp.bfloat16)
    grad_query = head_product("hqk,khc->qhc", grad_scores, key_heads).reshape(
        row_count, model_width
    ) * HEAD_DIM ** (-0.5)
    grad_keys = head_product("hqk,qhc->khc", grad_scores, query_heads).reshape(
        row_count, model_width
    )
    grad_query_bias = jnp.sum(grad_query, axis=0)
    grad_value_bias = jnp.sum(grad_values, axis=0)
    grad_proj = jnp.concatenate([grad_query, grad_keys, grad_values], axis=1).astype(jnp.bfloat16)
    grad_normed_one = jnp.dot(
        grad_proj, attn_part[: 3 * model_width], preferred_element_type=jnp.float32
    )
    back_one = jax.vjp(layer_norm, hidden, gain_one, shift_one)[1]
    grad_below, grad_gain_one, grad_shift_one = back_one(grad_normed_one)
    grad_below = grad_mid + grad_below
    stacked_left = jnp.concatenate(
        [
            jnp.pad(grad_proj, ((0, 0), (0, model_width))),
            jnp.pad(context, ((0, 0), (3 * model_width, 0))),
        ],
        axis=0,
    )
    stacked_right = jnp.concatenate([normed_one, grad_mid_bf], axis=0)
    grad_attn_w = scatter_rows(contract_first(stacked_left, stacked_right).astype(jnp.bfloat16))
    grad_vector = jnp.concatenate(
        [
            grad_gain_one,
            grad_shift_one,
            grad_query_bias,
            grad_value_bias,
            grad_out_bias,
            grad_gain_two,
            grad_shift_two,
            grad_down_bias,
            grad_up_bias,
        ]
    )
    grad_vec_own = lax.psum_scatter(
        grad_vector.reshape(lax.axis_size(AXES), 1, -1), AXES, scatter_dimension=0, tiled=True
    )[0]
    return (grad_below, grad_attn_w, grad_up_w, grad_down_w, grad_vec_own)


def shards(tokens, seq_ends, attn_weight, up_weight, down_weight, vectors, cotangent):
    allowed = causal_mask(seq_ends[0], tokens.shape[0])
    params = (
        gather_rows(attn_weight[0]),
        gather_relative(up_weight[0]),
        gather_relative(down_weight[0]),
        gather_rows(vectors[0].reshape(1, 1, -1)).reshape(-1),
    )
    hidden, saved_acts = forward_layer(tokens.astype(jnp.float32), params, allowed)
    output = hidden.astype(jnp.bfloat16)
    grad_tokens, grad_attn, grad_up, grad_down, grad_vectors = backward_layer(
        cotangent.astype(jnp.float32), params, saved_acts, allowed
    )
    return (output, grad_tokens, grad_attn[None], grad_up[None], grad_down[None], grad_vectors)


def solution(mesh):
    return jax.shard_map(
        shards,
        mesh=mesh,
        in_specs=(
            P(("dp", "shard"), None),
            P(("dp", "shard"), None),
            P(None, ("dp", "shard"), None),
            P(None, ("dp", "shard"), None),
            P(None, ("dp", "shard"), None),
            P(None, ("dp", "shard")),
            P(("dp", "shard"), None),
        ),
        out_specs=(
            P(("dp", "shard"), None),
            P(("dp", "shard"), None),
            P(None, ("dp", "shard"), None),
            P(None, ("dp", "shard"), None),
            P(None, ("dp", "shard"), None),
            P(None, ("dp", "shard")),
        ),
        check_vma=False,
    )
```

```python
import jax
import jax.numpy as jnp
from jax import lax
from jax.sharding import PartitionSpec as P

HEAD_DIM = 64


EPS = 1e-05
AXES = ("dp", "shard")


CORE, SIDE, ACROSS, LINE = 2, 1, 4, 8


def exchange(values, mask):
    pairs = [(source, source ^ mask) for source in range(lax.axis_size(AXES))]
    return lax.ppermute(values, AXES, pairs)


def gather_rows(values):
    return lax.all_gather(values, AXES, axis=0, tiled=True)


def scatter_rows(values):
    return lax.psum_scatter(values, AXES, scatter_dimension=0, tiled=True).astype(jnp.float32)


def relative_order(device_count):
    lines = list(range(0, device_count, LINE))
    orders = []
    for masks, steps in (
        (lines[: len(lines) // 2], (ACROSS, SIDE)),
        (lines[len(lines) // 2 :], (SIDE, ACROSS)),
    ):
        for step in steps:
            masks = masks + [mask ^ step for mask in masks]
        orders.append(masks)
    both = orders[0] + orders[1]
    return both + [mask ^ CORE for mask in both]


def gather_relative(block):
    device_count = lax.axis_size(AXES)
    lines = [block] + [exchange(block, mask) for mask in range(LINE, device_count, LINE)]
    pieces = []
    for members, steps in (
        (lines[: len(lines) // 2], (ACROSS, SIDE)),
        (lines[len(lines) // 2 :], (SIDE, ACROSS)),
    ):
        piece = jnp.concatenate(members, axis=0)
        for step in steps:
            piece = jnp.concatenate([piece, exchange(piece, step)], axis=0)
        pieces.append(piece)
    return pieces + [exchange(piece, CORE) for piece in pieces]


def add_rounded(left, right):
    return (left.astype(jnp.float32) + right.astype(jnp.float32)).astype(jnp.bfloat16)


def scatter_first(left, right):
    piece_rows = left.shape[1] // 4
    cuts = [left[:, piece * piece_rows : (piece + 1) * piece_rows] for piece in range(4)]
    away = [exchange(contract_first(cut, right).astype(jnp.bfloat16), CORE) for cut in cuts[2:]]
    return cuts[:2], away


def scatter_half(cuts, right, away):
    kept, received = [], []
    for cut, arrived, step in zip(cuts, away, (SIDE, ACROSS)):
        piece = (contract_first(cut, right) + arrived.astype(jnp.float32)).astype(jnp.bfloat16)
        half = piece.shape[0] // 2
        kept.append(piece[:half])
        received.append(exchange(piece[half:], step))
    return kept, received


def scatter_last(kept, received, block_rows):
    lines = []
    for own, arrived, step in zip(kept, received, (ACROSS, SIDE)):
        piece = add_rounded(own, arrived)
        half = piece.shape[0] // 2
        piece = add_rounded(piece[:half], exchange(piece[half:], step))
        lines += [
            piece[start : start + block_rows] for start in range(0, piece.shape[0], block_rows)
        ]
    total = lines[0].astype(jnp.float32)
    for index in range(1, len(lines)):
        total = total + exchange(lines[index], index * LINE).astype(jnp.float32)
    return total


def to_relative(values):
    device_count = lax.axis_size(AXES)
    order = jnp.array(relative_order(device_count), jnp.int32)
    blocks = values.reshape(device_count, -1)
    return blocks[order ^ lax.axis_index(AXES)].reshape(-1)


def from_relative(values):
    device_count = lax.axis_size(AXES)
    order = relative_order(device_count)
    place = jnp.array([order.index(mask) for mask in range(device_count)], jnp.int32)
    device = jnp.arange(device_count, dtype=jnp.int32) ^ lax.axis_index(AXES)
    return values.reshape(device_count, -1)[place[device]].reshape(-1)


def scatter_vector(values):
    blocks = to_relative(values).reshape(lax.axis_size(AXES), -1)
    half = blocks.shape[0] // 2
    blocks = blocks[:half] + exchange(blocks[half:], CORE)
    half = half // 2
    lines = []
    for piece, steps in ((blocks[:half], (SIDE, ACROSS)), (blocks[half:], (ACROSS, SIDE))):
        for step in steps:
            kept = piece.shape[0] // 2
            piece = piece[:kept] + exchange(piece[kept:], step)
        lines += [piece[row : row + 1] for row in range(piece.shape[0])]
    total = lines[0]
    for index in range(1, len(lines)):
        total = total + exchange(lines[index], index * LINE)
    return total


def contract_last_pieces(left, pieces):
    return jnp.concatenate([contract_last(left, piece) for piece in pieces], axis=1)


def dot_pieces(left, pieces):
    rows = pieces[0].shape[0]
    total = None
    for index, piece in enumerate(pieces):
        term = jnp.dot(
            left[:, index * rows : (index + 1) * rows], piece, preferred_element_type=jnp.float32
        )
        total = term if total is None else total + term
    return total


def layer_norm(values, gain, shift):
    average = jnp.mean(values, axis=-1, keepdims=True)
    centred = values - average
    variance = jnp.mean(centred * centred, axis=-1, keepdims=True)
    return centred * lax.rsqrt(variance + EPS) * gain + shift


def gelu_tanh(values):
    return (
        0.5
        * values
        * (1.0 + jnp.tanh(0.7978845608028654 * (values + 0.044715 * values * values * values)))
    )


def contract_last(left, right):
    return lax.dot_general(
        left, right, (((1,), (1,)), ((), ())), preferred_element_type=jnp.float32
    )


def contract_first(left, right):
    return lax.dot_general(
        left, right, (((0,), (0,)), ((), ())), preferred_element_type=jnp.float32
    )


def head_product(form, left, right):
    return jnp.einsum(form, left, right, preferred_element_type=jnp.float32)


def causal_mask(ends_row, slot_count):
    positions = jnp.arange(slot_count, dtype=jnp.int32)
    segment = jnp.sum((ends_row[None, :] <= positions[:, None]).astype(jnp.int32), axis=1)
    return (segment[:, None] == segment[None, :]) & (positions[None, :] <= positions[:, None])


def split_vectors(vectors, model_width):
    vector_f32 = vectors.astype(jnp.float32)
    parts_list = [
        vector_f32[slot_idx * model_width : (slot_idx + 1) * model_width] for slot_idx in range(8)
    ]
    return parts_list + [vector_f32[8 * model_width :]]


def forward_layer(hidden, params, allowed):
    attn_part, up_part, down_part, vector_part = params
    model_width = attn_part.shape[1]
    head_count = model_width // HEAD_DIM
    row_count = hidden.shape[0]
    (
        gain_one,
        shift_one,
        query_bias,
        value_bias,
        out_bias,
        gain_two,
        shift_two,
        down_bias,
        up_bias,
    ) = split_vectors(vector_part, model_width)
    normed_one = layer_norm(hidden, gain_one, shift_one).astype(jnp.bfloat16)
    projected = contract_last(normed_one, attn_part[: 3 * model_width])
    query_heads = (
        ((projected[:, :model_width] + query_bias) * HEAD_DIM ** (-0.5))
        .astype(jnp.bfloat16)
        .reshape(row_count, head_count, HEAD_DIM)
    )
    key_heads = (
        projected[:, model_width : 2 * model_width]
        .astype(jnp.bfloat16)
        .reshape(row_count, head_count, HEAD_DIM)
    )
    value_heads = (
        (projected[:, 2 * model_width :] + value_bias)
        .astype(jnp.bfloat16)
        .reshape(row_count, head_count, HEAD_DIM)
    )
    scores = jnp.where(allowed[None], head_product("qhc,khc->hqk", query_heads, key_heads), -1e30)
    log_total = jnp.log(jnp.sum(jnp.exp(scores), axis=-1))
    weights = jnp.exp(scores - log_total[..., None]).astype(jnp.bfloat16)
    context = (
        head_product("hqk,khc->qhc", weights, value_heads)
        .reshape(row_count, model_width)
        .astype(jnp.bfloat16)
    )
    after_attn = (
        hidden
        + jnp.dot(context, attn_part[3 * model_width :], preferred_element_type=jnp.float32)
        + out_bias
    )
    normed_two = layer_norm(after_attn, gain_two, shift_two).astype(jnp.bfloat16)
    up_bias = to_relative(up_bias)
    pre_act = contract_last_pieces(normed_two, up_part) + up_bias
    activated = gelu_tanh(pre_act).astype(jnp.bfloat16)
    result = (
        after_attn + dot_pieces(activated, down_part) + down_bias
    )
    saved_acts = (
        hidden,
        normed_one,
        query_heads,
        key_heads,
        value_heads,
        log_total,
        context,
        after_attn,
        normed_two,
        pre_act,
        activated,
    )
    return (result, saved_acts)


def backward_layer(upstream, params, saved_acts, allowed):
    attn_part, up_part, down_part, vector_part = params
    (
        hidden,
        normed_one,
        query_heads,
        key_heads,
        value_heads,
        log_total,
        context,
        after_attn,
        normed_two,
        pre_act,
        activated,
    ) = saved_acts
    model_width = attn_part.shape[1]
    head_count = model_width // HEAD_DIM
    row_count = hidden.shape[0]
    (
        gain_one,
        shift_one,
        query_bias,
        value_bias,
        out_bias,
        gain_two,
        shift_two,
        down_bias,
        up_bias,
    ) = split_vectors(vector_part, model_width)
    device_count = lax.axis_size(AXES)
    block_rows = pre_act.shape[1] // device_count
    upstream_bf = upstream.astype(jnp.bfloat16)
    down_cuts, down_away = scatter_first(activated, upstream_bf)
    grad_down_bias = jnp.sum(upstream, axis=0)
    grad_act = contract_last_pieces(upstream_bf, down_part)
    grad_pre = jax.vjp(gelu_tanh, pre_act)[1](grad_act)[0]
    grad_up_bias = from_relative(jnp.sum(grad_pre, axis=0))
    grad_pre_bf = grad_pre.astype(jnp.bfloat16)
    down_away, grad_pre_bf = lax.optimization_barrier((down_away, grad_pre_bf))
    down_kept, down_received = scatter_half(down_cuts, upstream_bf, down_away)
    up_cuts, up_away = scatter_first(grad_pre_bf, normed_two)
    grad_normed_two = dot_pieces(grad_pre_bf, up_part)
    back_two = jax.vjp(layer_norm, after_attn, gain_two, shift_two)[1]
    grad_mid, grad_gain_two, grad_shift_two = back_two(grad_normed_two)
    grad_mid = upstream + grad_mid
    grad_out_bias = jnp.sum(grad_mid, axis=0)
    grad_mid_bf = grad_mid.astype(jnp.bfloat16)
    grad_context = (
        contract_last(grad_mid_bf, attn_part[3 * model_width :])
        .astype(jnp.bfloat16)
        .reshape(row_count, head_count, HEAD_DIM)
    )
    up_away, grad_context = lax.optimization_barrier((up_away, grad_context))
    up_kept, up_received = scatter_half(up_cuts, normed_two, up_away)
    scores = jnp.where(allowed[None], head_product("qhc,khc->hqk", query_heads, key_heads), -1e30)
    probs_f32 = jnp.exp(scores - log_total[..., None])
    probs_bf = probs_f32.astype(jnp.bfloat16)
    grad_values = head_product("hqk,qhc->khc", probs_bf, grad_context).reshape(
        row_count, model_width
    )
    grad_probs = head_product("qhc,khc->hqk", grad_context, value_heads)
    row_dot = jnp.sum(probs_f32 * grad_probs, axis=-1, keepdims=True)
    grad_scores = (probs_f32 * (grad_probs - row_dot)).astype(jnp.bfloat16)
    grad_query = head_product("hqk,khc->qhc", grad_scores, key_heads).reshape(
        row_count, model_width
    ) * HEAD_DIM ** (-0.5)
    grad_keys = head_product("hqk,qhc->khc", grad_scores, query_heads).reshape(
        row_count, model_width
    )
    grad_query_bias = jnp.sum(grad_query, axis=0)
    grad_value_bias = jnp.sum(grad_values, axis=0)
    grad_proj = jnp.concatenate([grad_query, grad_keys, grad_values], axis=1).astype(jnp.bfloat16)
    down_received, grad_proj = lax.optimization_barrier((down_received, grad_proj))
    grad_down_w = scatter_last(down_kept, down_received, block_rows)
    grad_up_w = scatter_last(up_kept, up_received, block_rows)
    grad_normed_one = jnp.dot(
        grad_proj, attn_part[: 3 * model_width], preferred_element_type=jnp.float32
    )
    back_one = jax.vjp(layer_norm, hidden, gain_one, shift_one)[1]
    grad_below, grad_gain_one, grad_shift_one = back_one(grad_normed_one)
    grad_below = grad_mid + grad_below
    stacked_left = jnp.concatenate(
        [
            jnp.pad(grad_proj, ((0, 0), (0, model_width))),
            jnp.pad(context, ((0, 0), (3 * model_width, 0))),
        ],
        axis=0,
    )
    stacked_right = jnp.concatenate([normed_one, grad_mid_bf], axis=0)
    grad_attn_w = scatter_rows(contract_first(stacked_left, stacked_right).astype(jnp.bfloat16))
    grad_vector = jnp.concatenate(
        [
            grad_gain_one,
            grad_shift_one,
            grad_query_bias,
            grad_value_bias,
            grad_out_bias,
            grad_gain_two,
            grad_shift_two,
            grad_down_bias,
            grad_up_bias,
        ]
    )
    grad_vec_own = scatter_vector(grad_vector)
    return (grad_below, grad_attn_w, grad_up_w, grad_down_w, grad_vec_own)


def shards(tokens, seq_ends, attn_weight, up_weight, down_weight, vectors, cotangent):
    allowed = causal_mask(seq_ends[0], tokens.shape[0])
    params = (
        gather_rows(attn_weight[0]),
        gather_relative(up_weight[0]),
        gather_relative(down_weight[0]),
        from_relative(jnp.concatenate(gather_relative(vectors[0].reshape(1, -1)), axis=0)),
    )
    hidden, saved_acts = forward_layer(tokens.astype(jnp.float32), params, allowed)
    output = hidden.astype(jnp.bfloat16)
    grad_tokens, grad_attn, grad_up, grad_down, grad_vectors = backward_layer(
        cotangent.astype(jnp.float32), params, saved_acts, allowed
    )
    return (output, grad_tokens, grad_attn[None], grad_up[None], grad_down[None], grad_vectors)


def solution(mesh):
    return jax.shard_map(
        shards,
        mesh=mesh,
        in_specs=(
            P(("dp", "shard"), None),
            P(("dp", "shard"), None),
            P(None, ("dp", "shard"), None),
            P(None, ("dp", "shard"), None),
            P(None, ("dp", "shard"), None),
            P(None, ("dp", "shard")),
            P(("dp", "shard"), None),
        ),
        out_specs=(
            P(("dp", "shard"), None),
            P(("dp", "shard"), None),
            P(None, ("dp", "shard"), None),
            P(None, ("dp", "shard"), None),
            P(None, ("dp", "shard"), None),
            P(None, ("dp", "shard")),
        ),
        check_vma=False,
    )
```
